256 devices in a mesh: ctx: 32 (over y_lo, z, core), head: 8 (over y_hi, x).
Axes of the slice: x: 4, y: 4 (y_hi: 2, y_lo: 2; y = y_hi * 2 + y_lo), z: 8, core: 2. Of those that a mesh axis runs over, the one named last changes fastest.
Arguments:
- queries: bfloat16 [12288, 8, 6, 128], P('ctx', 'head'), may hold values from -5 to 5
- keys: bfloat16 [12288, 8, 128], P('ctx', 'head'), may hold values from -5 to 5
- values: bfloat16 [12288, 8, 128], P('ctx', 'head'), may hold values from -6 to 6
- d_out: bfloat16 [12288, 8, 6, 128], P('ctx', 'head'), may hold values from -45 to 45
- doc_block: int32 [96], replicated, may hold values from 0 to 23, never falling along the last dimension, each value on 1 to 12 neighbouring positions
- forget_flag: int32 [12288], P('ctx'), may hold values 0 or 1
Outputs:
- grad_queries: bfloat16 [12288, 8, 6, 128], P('ctx', 'head')
- grad_keys: bfloat16 [12288, 8, 128], P('ctx', 'head')
- grad_values: bfloat16 [12288, 8, 128], P('ctx', 'head')
The draws below stay inside these ranges and needn't reach their ends.
Inputs may be any that keep to these rules, and one draw needn't show every extreme that they name: `doc_block`: document ids never fall along the blocks; each document spans 1 to 12 blocks, and one spans exactly 12.
All inputs are finite; a program needn't handle non-finite values. No bound on the sum of `forget_flag` on one device may be relied on, other than what follows from the above.
Results may differ from the reference program's by a relative error of at most 0.0075.
Values may be sent and summed in bfloat16 or wider, within the bound.
No kernel may reach another device: no remote copies, remote signals or barrier semaphores. Data moves between devices by JAX's collectives and lax.ppermute only.
A program may use at most 128 MiB of HBM per device.

```python
import math
import jax
import jax.numpy as jnp
import numpy as np
from jax import lax

KVH = 8
G = 6
HD = 128
BLOCK = 128
DOCBLK = 12
SEQ = 12288
NBLK = 96
DOCMAX = 1536


def query_key_parts(key):
    base = jax.random.fold_in(key, 7)
    seed_query, seed_keys = jax.random.split(base, 2)
    rand_query = jnp.clip(jax.random.normal(seed_query, (SEQ, KVH, G, HD), jnp.float32), -4.5, 4.5)
    rand_keys = jnp.clip(jax.random.normal(seed_keys, (SEQ, KVH, HD), jnp.float32), -4.5, 4.5)
    return (rand_query, rand_keys)


def draw_queries(key, part):
    return query_key_parts(key)[0].astype(jnp.bfloat16)


def draw_keys(key, part):
    return query_key_parts(key)[1].astype(jnp.bfloat16)


def draw_d_out(key, part):
    base = jax.random.fold_in(key, 13)
    seed_main = jax.random.fold_in(base, 0)
    position = jnp.arange(SEQ, dtype=jnp.float32) / (SEQ - 1)
    head_frac = jnp.arange(KVH, dtype=jnp.float32) / (KVH - 1)
    values_raw = jnp.clip(jax.random.normal(seed_main, (SEQ, KVH, G, HD), jnp.float32), -4.0, 4.0)
    row_scale = jnp.exp(math.log(3.0) * position)
    head_scale = jnp.exp(math.log(3.5) * head_frac)
    scaled = values_raw * row_scale[:, None, None, None] * head_scale[None, :, None, None]
    return scaled.astype(jnp.bfloat16)


def touch_ends(values, stream_key, smallest, high):
    extent = values.shape
    spot = [jax.random.randint(jax.random.fold_in(stream_key, axis), (), 0, extent[axis]) for axis in range(len(extent))]
    values = values.at[tuple(spot)].set(smallest)
    longest = extent.index(max(extent))
    spot[longest] = (spot[longest] + 1) % extent[longest]
    return values.at[tuple(spot)].set(high)


def levels(rng, shape, shards, smallest, largest):
    gain = 1.0
    for dim, parts in shards:
        draws = jax.random.uniform(jax.random.fold_in(jax.random.fold_in(rng, 6), dim), (parts,), jnp.float32, smallest / len(shards), largest / len(shards))
        gain = gain * jnp.repeat(jnp.exp(draws), shape[dim] // parts).reshape((-1,) + (1,) * (len(shape) - 1 - dim))
    return gain


def length_profile(amount, total, limit, skew):
    portions = [(1 << 20) // math.isqrt(rank ** skew) + 1 for rank in range(2, amount + 1)]
    surplus, holding = total - limit - (amount - 1), [1] * (amount - 1)
    while surplus > 0:
        candidates = [i for i in range(amount - 1) if holding[i] < limit]
        whole, remaining = sum([portions[i] for i in candidates]), surplus
        for i in candidates:
            extra = min(limit - holding[i], max(1, remaining * portions[i] // whole), surplus)
            holding[i] = holding[i] + extra
            surplus = surplus - extra
    return np.array([limit] + holding)


def uneven(rng, count, total, limit, lean):
    if count == 2:
        one = jax.random.randint(rng, (), max(1, total - limit), min(limit, total - 1) + 1)
        return jnp.stack([one, total - one])
    lengths = jnp.asarray(length_profile(count, total, limit, lean), jnp.int32)
    couples = (count - 1) // 2
    source_of, receiver = lengths[1:1 + 2 * couples:2], lengths[2:2 + 2 * couples:2]
    room = jnp.minimum(source_of - 1, limit - receiver)
    passed = jax.random.randint(jax.random.fold_in(rng, 1), (couples,), 0, 1 << 20) % (room + 1)
    lengths = lengths.at[1:1 + 2 * couples:2].set(source_of - passed).at[2:2 + 2 * couples:2].set(receiver + passed)
    return lengths[jax.random.permutation(jax.random.fold_in(rng, 2), count)]


def centred(key, extent, width, reach, cuts=(), held_as=jnp.bfloat16):
    level = levels(key, extent, cuts, -0.22, 0.18) if cuts else 1.0
    array = jax.random.normal(key, extent, jnp.float32) * width * level
    return jnp.minimum(jnp.maximum(array, -reach), reach).astype(held_as)


def setup_inputs(seed: int = 0) -> dict:
    streams_of = jax.random.split(jax.random.key(seed), 7)
    queries = draw_queries(jax.random.fold_in(streams_of[6], 71), 0)
    keys = draw_keys(jax.random.fold_in(streams_of[6], 71), 0)
    values = centred(streams_of[2], (SEQ, KVH, HD), 1.0, 6.0, ((0, 32), (1, 8)))
    d_out = draw_d_out(jax.random.fold_in(streams_of[6], 71), 0)
    doc_block = jnp.searchsorted(jnp.cumsum(uneven(streams_of[4], NBLK // 4, NBLK, DOCBLK, 1)), jnp.arange(NBLK), side="right").astype(jnp.int32)
    forget_flag = touch_ends((jax.random.randint(streams_of[5], (SEQ,), 0, 4) < 1).astype(jnp.int32), jax.random.fold_in(streams_of[5], 1), 0, 1)
    return dict(queries=queries, keys=keys, values=values, d_out=d_out, doc_block=doc_block, forget_flag=forget_flag)


def to_half(value):
    return lax.optimization_barrier(value.astype(jnp.bfloat16)).astype(jnp.float32)

def reference(queries, keys, values, d_out, doc_block, forget_flag):
    softmax_scale = 1.0 / math.sqrt(HD)
    margin = DOCMAX - BLOCK
    sign_rows = (1 - 2 * forget_flag).astype(jnp.bfloat16)
    out_grad = d_out * sign_rows[:, None, None, None]
    token_doc = jnp.repeat(doc_block.astype(jnp.int32), BLOCK, total_repeat_length=SEQ)
    key_pad = jnp.pad(keys, ((margin, 0), (0, 0), (0, 0)))
    value_pad = jnp.pad(values, ((margin, 0), (0, 0), (0, 0)))
    doc_pad = jnp.concatenate([jnp.full((margin,), -1, jnp.int32), token_doc])
    window_iota = jnp.arange(DOCMAX, dtype=jnp.int32)
    block_iota = jnp.arange(BLOCK, dtype=jnp.int32)

    def one_block(carry, index):
        key_acc, value_acc = carry
        first = (index * BLOCK).astype(jnp.int32)
        query_rows = lax.dynamic_slice_in_dim(queries, first, BLOCK, 0).astype(jnp.float32)
        grad_rows = lax.dynamic_slice_in_dim(out_grad, first, BLOCK, 0).astype(jnp.float32)
        key_win = lax.dynamic_slice_in_dim(key_pad, first, DOCMAX, 0).astype(jnp.float32)
        value_win = lax.dynamic_slice_in_dim(value_pad, first, DOCMAX, 0).astype(jnp.float32)
        doc_win = lax.dynamic_slice_in_dim(doc_pad, first, DOCMAX, 0)
        query_pos = first + block_iota
        key_pos = first - margin + window_iota
        query_doc = doc_block[index]
        allowed = (key_pos[None, :] <= query_pos[:, None]) & (key_pos[None, :] >= 0) & (doc_win[None, :] == query_doc)
        scores = jnp.einsum('qhgd,khd->qhgk', query_rows, key_win) * softmax_scale
        scores = jnp.where(allowed[:, None, None, :], scores, -jnp.inf)
        top_score = lax.optimization_barrier(jnp.max(scores, axis=-1))
        log_norm = top_score + jnp.log(lax.optimization_barrier(jnp.sum(jnp.exp(scores - top_score[..., None]), axis=-1)))
        prob_full = jnp.exp(scores - log_norm[..., None])
        slopes = jnp.einsum('qhgd,khd->qhgk', grad_rows, value_win)
        row_delta = lax.optimization_barrier(jnp.sum(prob_full * slopes, axis=-1))
        dscore = prob_full * (slopes - row_delta[..., None])
        prob_half = to_half(prob_full)
        dscore_half = to_half(dscore)
        query_part = jnp.einsum('qhgk,khd->qhgd', dscore_half, key_win) * softmax_scale
        key_part = jnp.einsum('qhgk,qhgd->khd', dscore_half, query_rows) * softmax_scale
        value_part = jnp.einsum('qhgk,qhgd->khd', prob_half, grad_rows)
        key_acc = lax.dynamic_update_slice_in_dim(key_acc, lax.dynamic_slice_in_dim(key_acc, first, DOCMAX, 0) + key_part, first, 0)
        value_acc = lax.dynamic_update_slice_in_dim(value_acc, lax.dynamic_slice_in_dim(value_acc, first, DOCMAX, 0) + value_part, first, 0)
        return ((key_acc, value_acc), query_part)
    empty = jnp.zeros((SEQ + margin, KVH, HD), jnp.float32)
    (key_acc, value_acc), query_blocks = lax.scan(one_block, (empty, empty), jnp.arange(NBLK, dtype=jnp.int32))
    query_sum = query_blocks.reshape(SEQ, KVH, G, HD)
    key_sum = key_acc[margin:]
    value_sum = value_acc[margin:]
    square_total = jnp.sum(query_sum * query_sum) + jnp.sum(key_sum * key_sum) + jnp.sum(value_sum * value_sum)
    entries = SEQ * HD * KVH * (G + 2)
    norm_factor = lax.rsqrt(square_total / entries + 1e-06)
    return ((query_sum * norm_factor).astype(jnp.bfloat16), (key_sum * norm_factor).astype(jnp.bfloat16), (value_sum * norm_factor).astype(jnp.bfloat16))
```

```python
import functools
import math

import jax
import jax.numpy as jnp
from jax import lax
from jax.experimental import pallas as pl
from jax.experimental.pallas import tpu as pltpu
from jax.sharding import PartitionSpec as P

BLOCK = 128
REACH = 4
LOW = -1e30
F32 = jnp.float32
BF16 = jnp.bfloat16
NT = (((1,), (1,)), ((), ()))


def attn_kernel(
    blocks,
    chunks,
    me_ref,
    doc_ref,
    q_ref,
    do_ref,
    sign_ref,
    own_kv,
    kv_two,
    kv_four,
    sib_own,
    sib_two,
    sib_four,
    dq_ref,
    own_ref,
    two_ref,
    four_ref,
    cross_ref,
    sq_ref,
    win_k,
    win_v,
    s_ref,
    d_ref,
    m_ref,
    l_ref,
    w_ref,
    p_half,
    ds_half,
    q_rows,
    do_rows,
    q_turned,
    do_turned,
    dq_acc,
    dk_acc,
    dv_acc,
    sems,
):
    groups, tok_rows, width = q_ref.shape
    rows = groups * BLOCK
    shard = tok_rows
    scale = 1.0 / math.sqrt(width)
    expo = scale * math.log2(math.e)
    me = me_ref[0]
    core = lax.rem(me, 2)

    def fetch(source, slot_start, sem_index):
        start = pl.multiple_of(slot_start * shard, BLOCK)
        return (
            pltpu.make_async_copy(
                source.at[0], win_k.at[pl.ds(start, shard)], sems.at[sem_index, 0]
            ),
            pltpu.make_async_copy(
                source.at[1], win_v.at[pl.ds(start, shard)], sems.at[sem_index, 1]
            ),
        )

    copies = []
    copies += fetch(own_kv, REACH, 0)
    copies += fetch(kv_two, REACH - 2, 1)
    copies += fetch(kv_four, REACH - 4, 2)
    copies += fetch(sib_two, jnp.where(core == 0, REACH - 1, REACH - 3), 3)
    for copy in copies:
        copy.start()

    @pl.when(core == 0)
    def _():
        pair = fetch(sib_four, REACH - 3, 4)
        for copy in pair:
            copy.start()
        for copy in pair:
            copy.wait()

    @pl.when(core == 1)
    def _():
        pair = fetch(sib_own, REACH - 1, 4)
        for copy in pair:
            copy.start()
        for copy in pair:
            copy.wait()

    dk_acc[...] = jnp.zeros_like(dk_acc)
    dv_acc[...] = jnp.zeros_like(dv_acc)
    sq_ref[...] = jnp.zeros_like(sq_ref)
    for copy in copies:
        copy.wait()

    def one_block(b, carry):
        tok = pl.multiple_of(b * BLOCK, BLOCK)
        global_block = me * blocks + b
        my_doc = doc_ref[global_block]
        span = jnp.int32(1)
        for back in range(1, 2 * chunks):
            source = jnp.maximum(global_block - back, 0)
            same = (global_block >= back) & (doc_ref[source] == my_doc)
            span = span + same.astype(jnp.int32)
        steps = (span + 1) // 2
        last_block = REACH * blocks + b
        first_block = last_block + 1 - span
        for g in range(groups):
            at = slice(g * BLOCK, (g + 1) * BLOCK)
            q_part = q_ref[g, pl.ds(tok, BLOCK), :]
            do_part = do_ref[g, pl.ds(tok, BLOCK), :]
            q_rows[at, :] = q_part
            do_rows[at, :] = do_part
            q_turned[:, at] = q_part.T
            do_turned[:, at] = do_part.T

        def chunk_rows(step):
            return pl.multiple_of((last_block - 1 - 2 * step) * BLOCK, BLOCK)

        def raw_scores(step):
            k_pair = win_k[pl.ds(chunk_rows(step), 2 * BLOCK), :]
            return lax.dot_general(q_rows[...], k_pair, NT, preferred_element_type=F32)

        first = raw_scores(0)
        key_at = lax.broadcasted_iota(jnp.int32, (BLOCK, BLOCK), 1)
        tok_at = lax.broadcasted_iota(jnp.int32, (BLOCK, BLOCK), 0)
        causal = key_at <= tok_at
        before = last_block - 1 >= first_block
        for g in range(groups):
            at = slice(g * BLOCK, (g + 1) * BLOCK)
            far = jnp.where(before, first[at, :BLOCK], LOW)
            near = jnp.where(causal, first[at, BLOCK:], LOW)
            s_ref[0, at, :BLOCK] = far
            s_ref[0, at, BLOCK:] = near
            m_ref[at, :] = jnp.maximum(far, near)

        def score_step(step, c):
            scores = raw_scores(step)
            whole = last_block - 1 - 2 * step >= first_block
            for g in range(groups):
                at = slice(g * BLOCK, (g + 1) * BLOCK)
                far = jnp.where(whole, scores[at, :BLOCK], LOW)
                near = scores[at, BLOCK:]
                s_ref[step, at, :BLOCK] = far
                s_ref[step, at, BLOCK:] = near
                m_ref[at, :] = jnp.maximum(m_ref[at, :], jnp.maximum(far, near))
            return c

        lax.fori_loop(1, steps, score_step, 0)
        for g in range(groups):
            at = slice(g * BLOCK, (g + 1) * BLOCK)
            top = jnp.max(m_ref[at, :], axis=1, keepdims=True)
            m_ref[at, :] = jnp.broadcast_to(top, (BLOCK, BLOCK))
        l_ref[...] = jnp.zeros_like(l_ref)
        w_ref[...] = jnp.zeros_like(w_ref)

        def expo_step(step, c):
            v_pair = win_v[pl.ds(chunk_rows(step), 2 * BLOCK), :]
            slopes = lax.dot_general(do_rows[...], v_pair, NT, preferred_element_type=F32)
            for g in range(groups):
                at = slice(g * BLOCK, (g + 1) * BLOCK)
                top = m_ref[at, :]
                far = jnp.exp2((s_ref[step, at, :BLOCK] - top) * expo)
                near = jnp.exp2((s_ref[step, at, BLOCK:] - top) * expo)
                s_ref[step, at, :BLOCK] = far
                s_ref[step, at, BLOCK:] = near
                far_slope = slopes[at, :BLOCK]
                near_slope = slopes[at, BLOCK:]
                d_ref[step, at, :BLOCK] = far_slope
                d_ref[step, at, BLOCK:] = near_slope
                l_ref[at, :] += far + near
                w_ref[at, :] += far * far_slope + near * near_slope
            return c

        lax.fori_loop(0, steps, expo_step, 0)
        for g in range(groups):
            at = slice(g * BLOCK, (g + 1) * BLOCK)
            total = jnp.sum(l_ref[at, :], axis=1, keepdims=True)
            weighted = jnp.sum(w_ref[at, :], axis=1, keepdims=True)
            inverse = 1.0 / total
            w_ref[at, :] = jnp.broadcast_to(weighted * inverse, (BLOCK, BLOCK))
            l_ref[at, :] = inverse * sign_ref[pl.ds(tok, BLOCK), :]
        dq_acc[...] = jnp.zeros_like(dq_acc)

        def grad_step(step, c):
            for g in range(groups):
                at = slice(g * BLOCK, (g + 1) * BLOCK)
                inverse = l_ref[at, :]
                delta = w_ref[at, :]
                for half in (slice(0, BLOCK), slice(BLOCK, 2 * BLOCK)):
                    prob = s_ref[step, at, half] * inverse
                    p_half[at, half] = prob.astype(BF16)
                    ds_half[at, half] = (prob * (d_ref[step, at, half] - delta)).astype(BF16)
            k_pair = win_k[pl.ds(chunk_rows(step), 2 * BLOCK), :]
            dq_acc[...] += jnp.dot(ds_half[...], k_pair, preferred_element_type=F32)
            k_turned = jnp.dot(q_turned[...], ds_half[...], preferred_element_type=F32)
            v_turned = jnp.dot(do_turned[...], p_half[...], preferred_element_type=F32)
            low_block = last_block - 1 - 2 * step
            dk_acc[low_block] += k_turned[:, :BLOCK]
            dk_acc[low_block + 1] += k_turned[:, BLOCK:]
            dv_acc[low_block] += v_turned[:, :BLOCK]
            dv_acc[low_block + 1] += v_turned[:, BLOCK:]
            return c

        lax.fori_loop(0, steps, grad_step, 0)
        squares = jnp.zeros((BLOCK, width), F32)
        for g in range(groups):
            at = slice(g * BLOCK, (g + 1) * BLOCK)
            part = dq_acc[at, :] * scale
            dq_ref[g, pl.ds(tok, BLOCK), :] = part
            squares = squares + part * part
        sq_ref[...] += jnp.sum(squares.reshape(BLOCK // 8, 8, width), axis=0)
        return carry

    lax.fori_loop(0, blocks, one_block, 0)

    def emit(ref, lead, start_block):
        for i in range(blocks):
            ref[(*lead, 0, i)] = (dk_acc[start_block + i] * scale).astype(ref.dtype)
            ref[(*lead, 1, i)] = dv_acc[start_block + i].astype(ref.dtype)

    emit(own_ref, (), REACH * blocks)
    emit(two_ref, (), (REACH - 2) * blocks)
    emit(four_ref, (), (REACH - 4) * blocks)
    emit(cross_ref, (0,), jnp.where(core == 0, REACH - 1, REACH - 3) * blocks)
    emit(cross_ref, (1,), jnp.where(core == 0, REACH - 3, REACH - 1) * blocks)


def combine_kernel(me_ref, two_ref, four_ref, cross_ref, two_out, four_out):
    core = lax.rem(me_ref[0], 2)
    two_out[...] = (two_ref[...].astype(F32) + cross_ref[0].astype(F32)).astype(BF16)
    for kind in range(2):
        for i in range(four_ref.shape[1]):
            more = jnp.where(core == 1, cross_ref[1, kind, i].astype(F32), 0.0)
            four_out[kind, i] = (four_ref[kind, i].astype(F32) + more).astype(BF16)


def total_kernel(me_ref, own_ref, two_ref, four_ref, cross_ref, sq_ref, kv_out, sent_ref):
    core = lax.rem(me_ref[0], 2)
    squares = jnp.zeros(own_ref.shape[2:], F32)
    for kind in range(2):
        for i in range(own_ref.shape[1]):
            more = jnp.where(core == 0, cross_ref[1, kind, i].astype(F32), 0.0)
            whole = own_ref[kind, i] + more
            whole = whole + two_ref[kind, i].astype(F32) + four_ref[kind, i].astype(F32)
            squares = squares + whole * whole
            kv_out[kind, i * BLOCK : (i + 1) * BLOCK, :] = whole.T
    local = jnp.sum(squares) + jnp.sum(sq_ref[...])
    sent_ref[...] = jnp.full(sent_ref.shape, local, F32)


def finish_kernel(entries, got_ref, dq_ref, kv_ref, gq_ref, gk_ref, gv_ref):
    got = got_ref[...]
    total = jnp.sum(got) / got.shape[-1]
    norm = lax.rsqrt(jnp.full((1, 1), total / entries + 1e-06, F32))
    for g in range(dq_ref.shape[0]):
        gq_ref[g] = (dq_ref[g] * norm).astype(BF16)
    gk_ref[...] = (kv_ref[0] * norm).astype(BF16)
    gv_ref[...] = (kv_ref[1] * norm).astype(BF16)


def whole_specs(count):
    return [pl.BlockSpec(memory_space=pltpu.VMEM)] * count


def body(queries, keys, values, d_out, doc_block, forget_flag):
    tok_rows, _, groups, width = queries.shape
    blocks = tok_rows // BLOCK
    ctx_count = lax.axis_size("ctx")
    device_count = ctx_count * lax.axis_size("head")
    me = lax.axis_index("ctx").astype(jnp.int32).reshape(1)
    chunks = REACH * blocks // 2
    rows = groups * BLOCK

    def shifted(x, by):
        pairs = [(i, i + by) for i in range(ctx_count) if 0 <= i + by < ctx_count]
        return lax.ppermute(x, "ctx", pairs)

    def sibling(x):
        return lax.ppermute(x, "ctx", [(i, i ^ 1) for i in range(ctx_count)])

    q = queries.transpose(1, 2, 0, 3).reshape(groups, tok_rows, width)
    do = d_out.transpose(1, 2, 0, 3).reshape(groups, tok_rows, width)
    kv = jnp.stack([keys.reshape(tok_rows, width), values.reshape(tok_rows, width)])
    sign = (1 - 2 * forget_flag).astype(F32)
    sign = jnp.broadcast_to(sign[:, None], (tok_rows, BLOCK))
    kv_two = shifted(kv, 2)
    kv_four = shifted(kv, 4)
    sib_own = sibling(kv)
    sib_two = sibling(kv_two)
    sib_four = sibling(kv_four)

    smem = pl.BlockSpec(memory_space=pltpu.SMEM)
    anywhere = pl.BlockSpec(memory_space=pl.ANY)
    part = (2, blocks, width, BLOCK)
    window = (REACH + 1) * tok_rows
    dq, own, two, four, cross, sq = pl.pallas_call(
        functools.partial(attn_kernel, blocks, chunks),
        out_shape=(
            jax.ShapeDtypeStruct((groups, tok_rows, width), F32),
            jax.ShapeDtypeStruct(part, F32),
            jax.ShapeDtypeStruct(part, BF16),
            jax.ShapeDtypeStruct(part, BF16),
            jax.ShapeDtypeStruct((2, *part), BF16),
            jax.ShapeDtypeStruct((8, width), F32),
        ),
        in_specs=[smem, smem, *whole_specs(3), *[anywhere] * 6],
        out_specs=tuple(whole_specs(6)),
        scratch_shapes=[
            pltpu.VMEM((window, width), BF16),
            pltpu.VMEM((window, width), BF16),
            pltpu.VMEM((chunks, rows, 2 * BLOCK), F32),
            pltpu.VMEM((chunks, rows, 2 * BLOCK), F32),
            pltpu.VMEM((rows, BLOCK), F32),
            pltpu.VMEM((rows, BLOCK), F32),
            pltpu.VMEM((rows, BLOCK), F32),
            pltpu.VMEM((rows, 2 * BLOCK), BF16),
            pltpu.VMEM((rows, 2 * BLOCK), BF16),
            pltpu.VMEM((rows, width), BF16),
            pltpu.VMEM((rows, width), BF16),
            pltpu.VMEM((width, rows), BF16),
            pltpu.VMEM((width, rows), BF16),
            pltpu.VMEM((rows, width), F32),
            pltpu.VMEM(((REACH + 1) * blocks, width, BLOCK), F32),
            pltpu.VMEM(((REACH + 1) * blocks, width, BLOCK), F32),
            pltpu.SemaphoreType.DMA((5, 2)),
        ],
        name="attn",
    )(me, doc_block, q, do, sign, kv, kv_two, kv_four, sib_own, sib_two, sib_four)

    cross_in = sibling(cross)
    two_sum, four_sum = pl.pallas_call(
        combine_kernel,
        out_shape=(jax.ShapeDtypeStruct(part, BF16), jax.ShapeDtypeStruct(part, BF16)),
        in_specs=[smem, *whole_specs(3)],
        out_specs=tuple(whole_specs(2)),
        name="combine",
    )(me, two, four, cross_in)
    four_in = shifted(four_sum, -4)
    two_in = shifted(two_sum, -2)
    kv_sum, sent = pl.pallas_call(
        total_kernel,
        out_shape=(
            jax.ShapeDtypeStruct((2, tok_rows, width), F32),
            jax.ShapeDtypeStruct((device_count, 1, 128), F32),
        ),
        in_specs=[smem, *whole_specs(5)],
        out_specs=tuple(whole_specs(2)),
        name="total",
    )(me, own, two_in, four_in, cross_in, sq)
    got = lax.all_to_all(sent, ("ctx", "head"), 0, 0, tiled=True)
    entries = tok_rows * width * (groups + 2) * device_count
    gq, gk, gv = pl.pallas_call(
        functools.partial(finish_kernel, entries),
        out_shape=(
            jax.ShapeDtypeStruct((groups, tok_rows, width), BF16),
            jax.ShapeDtypeStruct((tok_rows, width), BF16),
            jax.ShapeDtypeStruct((tok_rows, width), BF16),
        ),
        in_specs=whole_specs(3),
        out_specs=tuple(whole_specs(3)),
        name="finish",
    )(got, dq, kv_sum)
    return (
        gq.reshape(1, groups, tok_rows, width).transpose(2, 0, 1, 3),
        gk.reshape(tok_rows, 1, width),
        gv.reshape(tok_rows, 1, width),
    )


def solution(mesh):
    placed = (
        P("ctx", "head", None, None),
        P("ctx", "head", None),
        P("ctx", "head", None),
        P("ctx", "head", None, None),
        P(),
        P("ctx"),
    )
    return jax.shard_map(
        body,
        mesh=mesh,
        in_specs=placed,
        out_specs=(P("ctx", "head", None, None), P("ctx", "head", None), P("ctx", "head", None)),
        check_vma=False,
    )
```

```python
import functools
import math

import jax
import jax.numpy as jnp
from jax import lax
from jax.experimental import pallas as pl
from jax.experimental.pallas import tpu as pltpu
from jax.sharding import PartitionSpec as P

BLOCK = 128
REACH = 4
LOW = -1e30
F32 = jnp.float32
BF16 = jnp.bfloat16
NT = (((1,), (1,)), ((), ()))


def attn_kernel(
    blocks,
    chunks,
    me_ref,
    doc_ref,
    q_ref,
    do_ref,
    flag_ref,
    own_kv,
    kv_two,
    kv_four,
    sib_own,
    sib_two,
    sib_four,
    dq_ref,
    own_ref,
    two_ref,
    four_ref,
    cross_ref,
    sq_ref,
    win_k,
    win_v,
    s_ref,
    d_ref,
    m_ref,
    l_ref,
    w_ref,
    p_half,
    ds_half,
    q_rows,
    do_rows,
    q_turned,
    do_turned,
    dq_acc,
    dk_acc,
    dv_acc,
    sems,
):
    groups, tok_rows, width = q_ref.shape
    rows = groups * BLOCK
    shard = tok_rows
    scale = 1.0 / math.sqrt(width)
    expo = scale * math.log2(math.e)
    me = me_ref[0]
    core = lax.rem(me, 2)

    def fetch(source, slot_start, sem_index):
        start = pl.multiple_of(slot_start * shard, BLOCK)
        return (
            pltpu.make_async_copy(
                source.at[0], win_k.at[pl.ds(start, shard)], sems.at[sem_index, 0]
            ),
            pltpu.make_async_copy(
                source.at[1], win_v.at[pl.ds(start, shard)], sems.at[sem_index, 1]
            ),
        )

    copies = []
    copies += fetch(own_kv, REACH, 0)
    copies += fetch(kv_two, REACH - 2, 1)
    copies += fetch(kv_four, REACH - 4, 2)
    copies += fetch(sib_two, jnp.where(core == 0, REACH - 1, REACH - 3), 3)
    for copy in copies:
        copy.start()

    @pl.when(core == 0)
    def _():
        pair = fetch(sib_four, REACH - 3, 4)
        for copy in pair:
            copy.start()
        for copy in pair:
            copy.wait()

    @pl.when(core == 1)
    def _():
        pair = fetch(sib_own, REACH - 1, 4)
        for copy in pair:
            copy.start()
        for copy in pair:
            copy.wait()

    dk_acc[...] = jnp.zeros_like(dk_acc)
    dv_acc[...] = jnp.zeros_like(dv_acc)
    sq_ref[...] = jnp.zeros_like(sq_ref)
    for copy in copies:
        copy.wait()

    def one_block(b, carry):
        tok = pl.multiple_of(b * BLOCK, BLOCK)
        global_block = me * blocks + b
        my_doc = doc_ref[global_block]
        span = jnp.int32(1)
        for back in range(1, 2 * chunks):
            source = jnp.maximum(global_block - back, 0)
            same = (global_block >= back) & (doc_ref[source] == my_doc)
            span = span + same.astype(jnp.int32)
        steps = (span + 1) // 2
        last_block = REACH * blocks + b
        first_block = last_block + 1 - span
        for g in range(groups):
            at = slice(g * BLOCK, (g + 1) * BLOCK)
            q_part = q_ref[g, pl.ds(tok, BLOCK), :]
            do_part = do_ref[g, pl.ds(tok, BLOCK), :]
            q_rows[at, :] = q_part
            do_rows[at, :] = do_part
            q_turned[:, at] = q_part.T
            do_turned[:, at] = do_part.T

        def chunk_rows(step):
            return pl.multiple_of((last_block - 1 - 2 * step) * BLOCK, BLOCK)

        def raw_scores(step):
            k_pair = win_k[pl.ds(chunk_rows(step), 2 * BLOCK), :]
            return lax.dot_general(q_rows[...], k_pair, NT, preferred_element_type=F32)

        first = raw_scores(0)
        key_at = lax.broadcasted_iota(jnp.int32, (BLOCK, BLOCK), 1)
        tok_at = lax.broadcasted_iota(jnp.int32, (BLOCK, BLOCK), 0)
        causal = key_at <= tok_at
        before = last_block - 1 >= first_block
        for g in range(groups):
            at = slice(g * BLOCK, (g + 1) * BLOCK)
            far = jnp.where(before, first[at, :BLOCK], LOW)
            near = jnp.where(causal, first[at, BLOCK:], LOW)
            s_ref[0, at, :BLOCK] = far
            s_ref[0, at, BLOCK:] = near
            m_ref[at, :] = jnp.maximum(far, near)

        def score_step(step, c):
            scores = raw_scores(step)
            whole = last_block - 1 - 2 * step >= first_block
            for g in range(groups):
                at = slice(g * BLOCK, (g + 1) * BLOCK)
                far = jnp.where(whole, scores[at, :BLOCK], LOW)
                near = scores[at, BLOCK:]
                s_ref[step, at, :BLOCK] = far
                s_ref[step, at, BLOCK:] = near
                m_ref[at, :] = jnp.maximum(m_ref[at, :], jnp.maximum(far, near))
            return c

        lax.fori_loop(1, steps, score_step, 0)
        for g in range(groups):
            at = slice(g * BLOCK, (g + 1) * BLOCK)
            top = jnp.max(m_ref[at, :], axis=1, keepdims=True)
            m_ref[at, :] = jnp.broadcast_to(top, (BLOCK, BLOCK))
        l_ref[...] = jnp.zeros_like(l_ref)
        w_ref[...] = jnp.zeros_like(w_ref)

        def expo_step(step, c):
            v_pair = win_v[pl.ds(chunk_rows(step), 2 * BLOCK), :]
            slopes = lax.dot_general(do_rows[...], v_pair, NT, preferred_element_type=F32)
            for g in range(groups):
                at = slice(g * BLOCK, (g + 1) * BLOCK)
                top = m_ref[at, :]
                far = jnp.exp2((s_ref[step, at, :BLOCK] - top) * expo)
                near = jnp.exp2((s_ref[step, at, BLOCK:] - top) * expo)
                s_ref[step, at, :BLOCK] = far
                s_ref[step, at, BLOCK:] = near
                far_slope = slopes[at, :BLOCK]
                near_slope = slopes[at, BLOCK:]
                d_ref[step, at, :BLOCK] = far_slope
                d_ref[step, at, BLOCK:] = near_slope
                l_ref[at, :] += far + near
                w_ref[at, :] += far * far_slope + near * near_slope
            return c

        lax.fori_loop(0, steps, expo_step, 0)
        sign = jnp.broadcast_to((1 - 2 * flag_ref[b]).astype(F32), (BLOCK, BLOCK)).T
        for g in range(groups):
            at = slice(g * BLOCK, (g + 1) * BLOCK)
            total = jnp.sum(l_ref[at, :], axis=1, keepdims=True)
            weighted = jnp.sum(w_ref[at, :], axis=1, keepdims=True)
            inverse = 1.0 / total
            w_ref[at, :] = jnp.broadcast_to(weighted * inverse, (BLOCK, BLOCK))
            l_ref[at, :] = inverse * sign
        dq_acc[...] = jnp.zeros_like(dq_acc)

        def grad_step(step, c):
            for g in range(groups):
                at = slice(g * BLOCK, (g + 1) * BLOCK)
                inverse = l_ref[at, :]
                delta = w_ref[at, :]
                for half in (slice(0, BLOCK), slice(BLOCK, 2 * BLOCK)):
                    prob = s_ref[step, at, half] * inverse
                    p_half[at, half] = prob.astype(BF16)
                    ds_half[at, half] = (prob * (d_ref[step, at, half] - delta)).astype(BF16)
            k_pair = win_k[pl.ds(chunk_rows(step), 2 * BLOCK), :]
            dq_acc[...] += jnp.dot(ds_half[...], k_pair, preferred_element_type=F32)
            k_turned = jnp.dot(q_turned[...], ds_half[...], preferred_element_type=F32)
            v_turned = jnp.dot(do_turned[...], p_half[...], preferred_element_type=F32)
            low_block = last_block - 1 - 2 * step
            dk_acc[low_block] += k_turned[:, :BLOCK]
            dk_acc[low_block + 1] += k_turned[:, BLOCK:]
            dv_acc[low_block] += v_turned[:, :BLOCK]
            dv_acc[low_block + 1] += v_turned[:, BLOCK:]
            return c

        lax.fori_loop(0, steps, grad_step, 0)
        squares = jnp.zeros((BLOCK, width), F32)
        for g in range(groups):
            at = slice(g * BLOCK, (g + 1) * BLOCK)
            part = dq_acc[at, :] * scale
            dq_ref[g, pl.ds(tok, BLOCK), :] = part.astype(BF16)
            squares = squares + part * part
        sq_ref[...] += jnp.sum(squares.reshape(BLOCK // 8, 8, width), axis=0)
        return carry

    lax.fori_loop(0, blocks, one_block, 0)

    def emit(ref, lead, start_block):
        for i in range(blocks):
            ref[(*lead, 0, i)] = (dk_acc[start_block + i] * scale).astype(ref.dtype)
            ref[(*lead, 1, i)] = dv_acc[start_block + i].astype(ref.dtype)

    emit(own_ref, (), REACH * blocks)
    emit(two_ref, (), (REACH - 2) * blocks)
    emit(four_ref, (), (REACH - 4) * blocks)
    emit(cross_ref, (0,), jnp.where(core == 0, REACH - 1, REACH - 3) * blocks)
    emit(cross_ref, (1,), jnp.where(core == 0, REACH - 3, REACH - 1) * blocks)


def combine_kernel(me_ref, two_ref, four_ref, cross_ref, two_out, four_out):
    core = lax.rem(me_ref[0], 2)
    two_out[...] = (two_ref[...].astype(F32) + cross_ref[0].astype(F32)).astype(BF16)
    for kind in range(2):
        for i in range(four_ref.shape[1]):
            more = jnp.where(core == 1, cross_ref[1, kind, i].astype(F32), 0.0)
            four_out[kind, i] = (four_ref[kind, i].astype(F32) + more).astype(BF16)


def total_kernel(me_ref, own_ref, two_ref, four_ref, cross_ref, sq_ref, kv_out, sent_ref):
    core = lax.rem(me_ref[0], 2)
    squares = jnp.zeros(own_ref.shape[2:], F32)
    for kind in range(2):
        for i in range(own_ref.shape[1]):
            more = jnp.where(core == 0, cross_ref[1, kind, i].astype(F32), 0.0)
            whole = own_ref[kind, i] + more
            whole = whole + two_ref[kind, i].astype(F32) + four_ref[kind, i].astype(F32)
            squares = squares + whole * whole
            kv_out[kind, i * BLOCK : (i + 1) * BLOCK, :] = whole.T
    local = jnp.sum(squares) + jnp.sum(sq_ref[...])
    sent_ref[...] = jnp.full(sent_ref.shape, local, F32)


def finish_kernel(entries, got_ref, dq_ref, kv_ref, gq_ref, gk_ref, gv_ref):
    got = got_ref[...]
    total = jnp.sum(got) / got.shape[-1]
    norm = lax.rsqrt(jnp.full((1, 1), total / entries + 1e-06, F32))
    for g in range(dq_ref.shape[0]):
        gq_ref[g] = (dq_ref[g].astype(F32) * norm).astype(BF16)
    gk_ref[...] = (kv_ref[0] * norm).astype(BF16)
    gv_ref[...] = (kv_ref[1] * norm).astype(BF16)


def whole_specs(count):
    return [pl.BlockSpec(memory_space=pltpu.VMEM)] * count


def body(queries, keys, values, d_out, doc_block, forget_flag):
    tok_rows, _, groups, width = queries.shape
    blocks = tok_rows // BLOCK
    ctx_count = lax.axis_size("ctx")
    device_count = ctx_count * lax.axis_size("head")
    me = lax.axis_index("ctx").astype(jnp.int32).reshape(1)
    chunks = REACH * blocks // 2
    rows = groups * BLOCK

    def shifted(x, by):
        pairs = [(i, i + by) for i in range(ctx_count) if 0 <= i + by < ctx_count]
        return lax.ppermute(x, "ctx", pairs)

    def sibling(x):
        return lax.ppermute(x, "ctx", [(i, i ^ 1) for i in range(ctx_count)])

    q = queries.transpose(1, 2, 0, 3).reshape(groups, tok_rows, width)
    do = d_out.transpose(1, 2, 0, 3).reshape(groups, tok_rows, width)
    kv = jnp.stack([keys.reshape(tok_rows, width), values.reshape(tok_rows, width)])
    flag = forget_flag.reshape(blocks, 1, BLOCK)
    kv_two = shifted(kv, 2)
    kv_four = shifted(kv, 4)
    sib_own = sibling(kv)
    sib_two = sibling(kv_two)
    sib_four = sibling(kv_four)

    smem = pl.BlockSpec(memory_space=pltpu.SMEM)
    anywhere = pl.BlockSpec(memory_space=pl.ANY)
    part = (2, blocks, width, BLOCK)
    window = (REACH + 1) * tok_rows
    dq, own, two, four, cross, sq = pl.pallas_call(
        functools.partial(attn_kernel, blocks, chunks),
        out_shape=(
            jax.ShapeDtypeStruct((groups, tok_rows, width), BF16),
            jax.ShapeDtypeStruct(part, F32),
            jax.ShapeDtypeStruct(part, BF16),
            jax.ShapeDtypeStruct(part, BF16),
            jax.ShapeDtypeStruct((2, *part), BF16),
            jax.ShapeDtypeStruct((8, width), F32),
        ),
        in_specs=[smem, smem, *whole_specs(3), *[anywhere] * 6],
        out_specs=tuple(whole_specs(6)),
        scratch_shapes=[
            pltpu.VMEM((window, width), BF16),
            pltpu.VMEM((window, width), BF16),
            pltpu.VMEM((chunks, rows, 2 * BLOCK), F32),
            pltpu.VMEM((chunks, rows, 2 * BLOCK), F32),
            pltpu.VMEM((rows, BLOCK), F32),
            pltpu.VMEM((rows, BLOCK), F32),
            pltpu.VMEM((rows, BLOCK), F32),
            pltpu.VMEM((rows, 2 * BLOCK), BF16),
            pltpu.VMEM((rows, 2 * BLOCK), BF16),
            pltpu.VMEM((rows, width), BF16),
            pltpu.VMEM((rows, width), BF16),
            pltpu.VMEM((width, rows), BF16),
            pltpu.VMEM((width, rows), BF16),
            pltpu.VMEM((rows, width), F32),
            pltpu.VMEM(((REACH + 1) * blocks, width, BLOCK), F32),
            pltpu.VMEM(((REACH + 1) * blocks, width, BLOCK), F32),
            pltpu.SemaphoreType.DMA((5, 2)),
        ],
        name="attn",
    )(me, doc_block, q, do, flag, kv, kv_two, kv_four, sib_own, sib_two, sib_four)

    cross_in = sibling(cross)
    two_sum, four_sum = pl.pallas_call(
        combine_kernel,
        out_shape=(jax.ShapeDtypeStruct(part, BF16), jax.ShapeDtypeStruct(part, BF16)),
        in_specs=[smem, *whole_specs(3)],
        out_specs=tuple(whole_specs(2)),
        name="combine",
    )(me, two, four, cross_in)
    four_in = shifted(four_sum, -4)
    two_in = shifted(two_sum, -2)
    kv_sum, sent = pl.pallas_call(
        total_kernel,
        out_shape=(
            jax.ShapeDtypeStruct((2, tok_rows, width), F32),
            jax.ShapeDtypeStruct((device_count, 1, 128), F32),
        ),
        in_specs=[smem, *whole_specs(5)],
        out_specs=tuple(whole_specs(2)),
        name="total",
    )(me, own, two_in, four_in, cross_in, sq)
    got = lax.all_to_all(sent, ("ctx", "head"), 0, 0, tiled=True)
    entries = tok_rows * width * (groups + 2) * device_count
    gq, gk, gv = pl.pallas_call(
        functools.partial(finish_kernel, entries),
        out_shape=(
            jax.ShapeDtypeStruct((groups, tok_rows, width), BF16),
            jax.ShapeDtypeStruct((tok_rows, width), BF16),
            jax.ShapeDtypeStruct((tok_rows, width), BF16),
        ),
        in_specs=whole_specs(3),
        out_specs=tuple(whole_specs(3)),
        name="finish",
    )(got, dq, kv_sum)
    return (
        gq.reshape(1, groups, tok_rows, width).transpose(2, 0, 1, 3),
        gk.reshape(tok_rows, 1, width),
        gv.reshape(tok_rows, 1, width),
    )


def solution(mesh):
    placed = (
        P("ctx", "head", None, None),
        P("ctx", "head", None),
        P("ctx", "head", None),
        P("ctx", "head", None, None),
        P(),
        P("ctx"),
    )
    return jax.shard_map(
        body,
        mesh=mesh,
        in_specs=placed,
        out_specs=(P("ctx", "head", None, None), P("ctx", "head", None), P("ctx", "head", None)),
        check_vma=False,
    )
```

```python
import functools
import math

import jax
import jax.numpy as jnp
from jax import lax
from jax.experimental import pallas as pl
from jax.experimental.pallas import tpu as pltpu
from jax.sharding import PartitionSpec as P

BLOCK = 128
REACH = 4
LOW = -1e30
F32 = jnp.float32
BF16 = jnp.bfloat16
NT = (((1,), (1,)), ((), ()))


def attn_kernel(
    blocks,
    chunks,
    me_ref,
    doc_ref,
    q_ref,
    do_ref,
    flag_hbm,
    own_kv,
    kv_two,
    kv_four,
    sib_own,
    sib_two,
    sib_four,
    dq_ref,
    own_ref,
    two_ref,
    four_ref,
    cross_ref,
    sq_ref,
    win_k,
    win_v,
    flag_ref,
    s_ref,
    d_ref,
    m_ref,
    l_ref,
    w_ref,
    p_half,
    ds_half,
    q_rows,
    do_rows,
    q_turned,
    do_turned,
    dq_acc,
    dk_acc,
    dv_acc,
    sems,
):
    groups, tok_rows, width = q_ref.shape
    rows = groups * BLOCK
    shard = tok_rows
    scale = 1.0 / math.sqrt(width)
    expo = scale * math.log2(math.e)
    me = me_ref[0]
    core = lax.rem(me, 2)

    def fetch(source, slot_start, sem_index):
        start = pl.multiple_of(slot_start * shard, BLOCK)
        return (
            pltpu.make_async_copy(
                source.at[0], win_k.at[pl.ds(start, shard)], sems.at[sem_index, 0]
            ),
            pltpu.make_async_copy(
                source.at[1], win_v.at[pl.ds(start, shard)], sems.at[sem_index, 1]
            ),
        )

    copies = [pltpu.make_async_copy(flag_hbm, flag_ref, sems.at[5, 0])]
    copies += fetch(own_kv, REACH, 0)
    copies += fetch(kv_two, REACH - 2, 1)
    copies += fetch(kv_four, REACH - 4, 2)
    copies += fetch(sib_two, jnp.where(core == 0, REACH - 1, REACH - 3), 3)
    for copy in copies:
        copy.start()

    @pl.when(core == 0)
    def _():
        pair = fetch(sib_four, REACH - 3, 4)
        for copy in pair:
            copy.start()
        for copy in pair:
            copy.wait()

    @pl.when(core == 1)
    def _():
        pair = fetch(sib_own, REACH - 1, 4)
        for copy in pair:
            copy.start()
        for copy in pair:
            copy.wait()

    dk_acc[...] = jnp.zeros_like(dk_acc)
    dv_acc[...] = jnp.zeros_like(dv_acc)
    sq_ref[...] = jnp.zeros_like(sq_ref)
    for copy in copies:
        copy.wait()

    def one_block(b, carry):
        tok = pl.multiple_of(b * BLOCK, BLOCK)
        global_block = me * blocks + b
        my_doc = doc_ref[global_block]
        span = jnp.int32(1)
        for back in range(1, 2 * chunks):
            source = jnp.maximum(global_block - back, 0)
            same = (global_block >= back) & (doc_ref[source] == my_doc)
            span = span + same.astype(jnp.int32)
        steps = (span + 1) // 2
        last_block = REACH * blocks + b
        first_block = last_block + 1 - span
        for g in range(groups):
            at = slice(g * BLOCK, (g + 1) * BLOCK)
            q_part = q_ref[g, pl.ds(tok, BLOCK), :]
            do_part = do_ref[g, pl.ds(tok, BLOCK), :]
            q_rows[at, :] = q_part
            do_rows[at, :] = do_part
            q_turned[:, at] = q_part.T
            do_turned[:, at] = do_part.T

        def chunk_rows(step):
            return pl.multiple_of((last_block - 1 - 2 * step) * BLOCK, BLOCK)

        def raw_scores(step):
            k_pair = win_k[pl.ds(chunk_rows(step), 2 * BLOCK), :]
            return lax.dot_general(q_rows[...], k_pair, NT, preferred_element_type=F32)

        first = raw_scores(0)
        key_at = lax.broadcasted_iota(jnp.int32, (BLOCK, BLOCK), 1)
        tok_at = lax.broadcasted_iota(jnp.int32, (BLOCK, BLOCK), 0)
        causal = key_at <= tok_at
        before = last_block - 1 >= first_block
        for g in range(groups):
            at = slice(g * BLOCK, (g + 1) * BLOCK)
            far = jnp.where(before, first[at, :BLOCK], LOW)
            near = jnp.where(causal, first[at, BLOCK:], LOW)
            s_ref[0, at, :BLOCK] = far
            s_ref[0, at, BLOCK:] = near
            m_ref[at, :] = jnp.maximum(far, near)

        def score_step(step, c):
            scores = raw_scores(step)
            whole = last_block - 1 - 2 * step >= first_block
            for g in range(groups):
                at = slice(g * BLOCK, (g + 1) * BLOCK)
                far = jnp.where(whole, scores[at, :BLOCK], LOW)
                near = scores[at, BLOCK:]
                s_ref[step, at, :BLOCK] = far
                s_ref[step, at, BLOCK:] = near
                m_ref[at, :] = jnp.maximum(m_ref[at, :], jnp.maximum(far, near))
            return c

        lax.fori_loop(1, steps, score_step, 0)
        for g in range(groups):
            at = slice(g * BLOCK, (g + 1) * BLOCK)
            top = jnp.max(m_ref[at, :], axis=1, keepdims=True)
            m_ref[at, :] = jnp.broadcast_to(top, (BLOCK, BLOCK))
        l_ref[...] = jnp.zeros_like(l_ref)
        w_ref[...] = jnp.zeros_like(w_ref)

        def expo_step(step, c):
            v_pair = win_v[pl.ds(chunk_rows(step), 2 * BLOCK), :]
            slopes = lax.dot_general(do_rows[...], v_pair, NT, preferred_element_type=F32)
            for g in range(groups):
                at = slice(g * BLOCK, (g + 1) * BLOCK)
                top = m_ref[at, :]
                far = jnp.exp2((s_ref[step, at, :BLOCK] - top) * expo)
                near = jnp.exp2((s_ref[step, at, BLOCK:] - top) * expo)
                s_ref[step, at, :BLOCK] = far
                s_ref[step, at, BLOCK:] = near
                far_slope = slopes[at, :BLOCK]
                near_slope = slopes[at, BLOCK:]
                d_ref[step, at, :BLOCK] = far_slope
                d_ref[step, at, BLOCK:] = near_slope
                l_ref[at, :] += far + near
                w_ref[at, :] += far * far_slope + near * near_slope
            return c

        lax.fori_loop(0, steps, expo_step, 0)
        sign = jnp.broadcast_to((1 - 2 * flag_ref[pl.ds(tok, BLOCK)]).astype(F32)[None, :], (BLOCK, BLOCK)).T
        for g in range(groups):
            at = slice(g * BLOCK, (g + 1) * BLOCK)
            total = jnp.sum(l_ref[at, :], axis=1, keepdims=True)
            weighted = jnp.sum(w_ref[at, :], axis=1, keepdims=True)
            inverse = 1.0 / total
            w_ref[at, :] = jnp.broadcast_to(weighted * inverse, (BLOCK, BLOCK))
            l_ref[at, :] = inverse * sign
        dq_acc[...] = jnp.zeros_like(dq_acc)

        def grad_step(step, c):
            for g in range(groups):
                at = slice(g * BLOCK, (g + 1) * BLOCK)
                inverse = l_ref[at, :]
                delta = w_ref[at, :]
                for half in (slice(0, BLOCK), slice(BLOCK, 2 * BLOCK)):
                    prob = s_ref[step, at, half] * inverse
                    p_half[at, half] = prob.astype(BF16)
                    ds_half[at, half] = (prob * (d_ref[step, at, half] - delta)).astype(BF16)
            k_pair = win_k[pl.ds(chunk_rows(step), 2 * BLOCK), :]
            dq_acc[...] += jnp.dot(ds_half[...], k_pair, preferred_element_type=F32)
            k_turned = jnp.dot(q_turned[...], ds_half[...], preferred_element_type=F32)
            v_turned = jnp.dot(do_turned[...], p_half[...], preferred_element_type=F32)
            low_block = last_block - 1 - 2 * step
            dk_acc[low_block] += k_turned[:, :BLOCK]
            dk_acc[low_block + 1] += k_turned[:, BLOCK:]
            dv_acc[low_block] += v_turned[:, :BLOCK]
            dv_acc[low_block + 1] += v_turned[:, BLOCK:]
            return c

        lax.fori_loop(0, steps, grad_step, 0)
        squares = jnp.zeros((BLOCK, width), F32)
        for g in range(groups):
            at = slice(g * BLOCK, (g + 1) * BLOCK)
            part = dq_acc[at, :] * scale
            dq_ref[g, pl.ds(tok, BLOCK), :] = part.astype(BF16)
            squares = squares + part * part
        sq_ref[...] += jnp.sum(squares.reshape(BLOCK // 8, 8, width), axis=0)
        return carry

    lax.fori_loop(0, blocks, one_block, 0)

    def emit(ref, lead, start_block):
        for i in range(blocks):
            ref[(*lead, 0, i)] = (dk_acc[start_block + i] * scale).astype(ref.dtype)
            ref[(*lead, 1, i)] = dv_acc[start_block + i].astype(ref.dtype)

    emit(own_ref, (), REACH * blocks)
    emit(two_ref, (), (REACH - 2) * blocks)
    emit(four_ref, (), (REACH - 4) * blocks)
    emit(cross_ref, (0,), jnp.where(core == 0, REACH - 1, REACH - 3) * blocks)
    emit(cross_ref, (1,), jnp.where(core == 0, REACH - 3, REACH - 1) * blocks)


def combine_kernel(me_ref, two_ref, four_ref, cross_ref, two_out, four_out):
    core = lax.rem(me_ref[0], 2)
    two_out[...] = (two_ref[...].astype(F32) + cross_ref[0].astype(F32)).astype(BF16)
    for kind in range(2):
        for i in range(four_ref.shape[1]):
            more = jnp.where(core == 1, cross_ref[1, kind, i].astype(F32), 0.0)
            four_out[kind, i] = (four_ref[kind, i].astype(F32) + more).astype(BF16)


def total_kernel(me_ref, own_ref, two_ref, four_ref, cross_ref, sq_ref, kv_out, sent_ref):
    core = lax.rem(me_ref[0], 2)
    squares = jnp.zeros(own_ref.shape[2:], F32)
    for kind in range(2):
        for i in range(own_ref.shape[1]):
            more = jnp.where(core == 0, cross_ref[1, kind, i].astype(F32), 0.0)
            whole = own_ref[kind, i] + more
            whole = whole + two_ref[kind, i].astype(F32) + four_ref[kind, i].astype(F32)
            squares = squares + whole * whole
            kv_out[kind, i * BLOCK : (i + 1) * BLOCK, :] = whole.T
    local = jnp.sum(squares) + jnp.sum(sq_ref[...])
    sent_ref[...] = jnp.full(sent_ref.shape, local, F32)


def finish_kernel(entries, got_ref, dq_ref, kv_ref, gq_ref, gk_ref, gv_ref):
    got = got_ref[...]
    total = jnp.sum(got) / got.shape[-1]
    norm = lax.rsqrt(jnp.full((1, 1), total / entries + 1e-06, F32))
    for g in range(dq_ref.shape[0]):
        gq_ref[g] = (dq_ref[g].astype(F32) * norm).astype(BF16)
    gk_ref[...] = (kv_ref[0] * norm).astype(BF16)
    gv_ref[...] = (kv_ref[1] * norm).astype(BF16)


def whole_specs(count):
    return [pl.BlockSpec(memory_space=pltpu.VMEM)] * count


def body(queries, keys, values, d_out, doc_block, forget_flag):
    tok_rows, _, groups, width = queries.shape
    blocks = tok_rows // BLOCK
    ctx_count = lax.axis_size("ctx")
    device_count = ctx_count * lax.axis_size("head")
    me = lax.axis_index("ctx").astype(jnp.int32).reshape(1)
    chunks = REACH * blocks // 2
    rows = groups * BLOCK

    def shifted(x, by):
        pairs = [(i, i + by) for i in range(ctx_count) if 0 <= i + by < ctx_count]
        return lax.ppermute(x, "ctx", pairs)

    def sibling(x):
        return lax.ppermute(x, "ctx", [(i, i ^ 1) for i in range(ctx_count)])

    q = queries.transpose(1, 2, 0, 3).reshape(groups, tok_rows, width)
    do = d_out.transpose(1, 2, 0, 3).reshape(groups, tok_rows, width)
    kv = jnp.stack([keys.reshape(tok_rows, width), values.reshape(tok_rows, width)])
    kv_two = shifted(kv, 2)
    kv_four = shifted(kv, 4)
    sib_own = sibling(kv)
    sib_two = sibling(kv_two)
    sib_four = sibling(kv_four)

    smem = pl.BlockSpec(memory_space=pltpu.SMEM)
    anywhere = pl.BlockSpec(memory_space=pl.ANY)
    part = (2, blocks, width, BLOCK)
    window = (REACH + 1) * tok_rows
    dq, own, two, four, cross, sq = pl.pallas_call(
        functools.partial(attn_kernel, blocks, chunks),
        out_shape=(
            jax.ShapeDtypeStruct((groups, tok_rows, width), BF16),
            jax.ShapeDtypeStruct(part, F32),
            jax.ShapeDtypeStruct(part, BF16),
            jax.ShapeDtypeStruct(part, BF16),
            jax.ShapeDtypeStruct((2, *part), BF16),
            jax.ShapeDtypeStruct((8, width), F32),
        ),
        in_specs=[smem, smem, *whole_specs(2), *[anywhere] * 7],
        out_specs=tuple(whole_specs(6)),
        scratch_shapes=[
            pltpu.VMEM((window, width), BF16),
            pltpu.VMEM((window, width), BF16),
            pltpu.VMEM((tok_rows,), jnp.int32),
            pltpu.VMEM((chunks, rows, 2 * BLOCK), F32),
            pltpu.VMEM((chunks, rows, 2 * BLOCK), F32),
            pltpu.VMEM((rows, BLOCK), F32),
            pltpu.VMEM((rows, BLOCK), F32),
            pltpu.VMEM((rows, BLOCK), F32),
            pltpu.VMEM((rows, 2 * BLOCK), BF16),
            pltpu.VMEM((rows, 2 * BLOCK), BF16),
            pltpu.VMEM((rows, width), BF16),
            pltpu.VMEM((rows, width), BF16),
            pltpu.VMEM((width, rows), BF16),
            pltpu.VMEM((width, rows), BF16),
            pltpu.VMEM((rows, width), F32),
            pltpu.VMEM(((REACH + 1) * blocks, width, BLOCK), F32),
            pltpu.VMEM(((REACH + 1) * blocks, width, BLOCK), F32),
            pltpu.SemaphoreType.DMA((6, 2)),
        ],
        name="attn",
    )(me, doc_block, q, do, forget_flag, kv, kv_two, kv_four, sib_own, sib_two, sib_four)

    cross_in = sibling(cross)
    two_sum, four_sum = pl.pallas_call(
        combine_kernel,
        out_shape=(jax.ShapeDtypeStruct(part, BF16), jax.ShapeDtypeStruct(part, BF16)),
        in_specs=[smem, *whole_specs(3)],
        out_specs=tuple(whole_specs(2)),
        name="combine",
    )(me, two, four, cross_in)
    four_in = shifted(four_sum, -4)
    two_in = shifted(two_sum, -2)
    kv_sum, sent = pl.pallas_call(
        total_kernel,
        out_shape=(
            jax.ShapeDtypeStruct((2, tok_rows, width), F32),
            jax.ShapeDtypeStruct((device_count, 1, 128), F32),
        ),
        in_specs=[smem, *whole_specs(5)],
        out_specs=tuple(whole_specs(2)),
        name="total",
    )(me, own, two_in, four_in, cross_in, sq)
    got = lax.all_to_all(sent, ("ctx", "head"), 0, 0, tiled=True)
    entries = tok_rows * width * (groups + 2) * device_count
    gq, gk, gv = pl.pallas_call(
        functools.partial(finish_kernel, entries),
        out_shape=(
            jax.ShapeDtypeStruct((groups, tok_rows, width), BF16),
            jax.ShapeDtypeStruct((tok_rows, width), BF16),
            jax.ShapeDtypeStruct((tok_rows, width), BF16),
        ),
        in_specs=whole_specs(3),
        out_specs=tuple(whole_specs(3)),
        name="finish",
    )(got, dq, kv_sum)
    return (
        gq.reshape(1, groups, tok_rows, width).transpose(2, 0, 1, 3),
        gk.reshape(tok_rows, 1, width),
        gv.reshape(tok_rows, 1, width),
    )


def solution(mesh):
    placed = (
        P("ctx", "head", None, None),
        P("ctx", "head", None),
        P("ctx", "head", None),
        P("ctx", "head", None, None),
        P(),
        P("ctx"),
    )
    return jax.shard_map(
        body,
        mesh=mesh,
        in_specs=placed,
        out_specs=(P("ctx", "head", None, None), P("ctx", "head", None), P("ctx", "head", None)),
        check_vma=False,
    )
```
